512 devices in a mesh: seq: 64 (over z, x), vis: 8 (over y, core).
Axes of the slice: x: 4, y: 4, z: 16, core: 2. Of those that a mesh axis runs over, the one named last changes fastest.
Arguments:
- queries: bfloat16 [16384, 4096], P('seq', 'vis'), may hold values from -120 to 120
- keys: bfloat16 [256, 8, 512], P('seq', 'vis'), may hold values from -7 to 7
- values: bfloat16 [256, 8, 512], P('seq', 'vis'), may hold values from -6 to 6
- grad_out: bfloat16 [16384, 4096], P('seq', 'vis'), may hold values from -6 to 6
- block_map: int32 [64, 32], replicated, may hold values from 0 to 255, as said below
- block_count: int32 [64], replicated, may hold values from 24 to 32, as said below
Outputs:
- grad_queries: bfloat16 [16384, 4096], P('seq', 'vis')
- log_totals: float32 [32, 16384], P('vis', 'seq')
- grad_keys: bfloat16 [256, 8, 512], P('seq', 'vis')
- grad_values: bfloat16 [256, 8, 512], P('seq', 'vis')
The draws below stay inside these ranges and needn't reach their ends.
Inputs may be any that keep to these rules, and one draw needn't show every extreme that they name: `block_map`: block b belongs to seq index b // 4; the 32 blocks that one span names belong to 32 different seq indices. `block_count`: some span attends all 32 of its named blocks.
All inputs are finite; a program needn't handle non-finite values.
Results may differ from the reference program's by a relative error of at most 0.014.
Values may be sent and summed in bfloat16 or wider, within the bound.
A program may use at most 64 MiB of HBM per device.

```python
import math
import jax
import jax.numpy as jnp
from jax import lax

HEADS = 32
KV_HEADS = 4
HEAD_DIM = 128
BLK = 8
TOK_DEV = 256
BPD = 4
GROUP = 8
HCOL = 4096
KVCOL = 512
NB = 32
NBLK = 256
TEXT = 16384
N_SEQ = 64


def block_table(key):
    base_key = jax.random.fold_in(key, 101)
    span_keys = jax.random.split(base_key, N_SEQ)
    owners = jax.vmap(lambda span_key: jax.random.permutation(span_key, N_SEQ)[:NB])(span_keys)
    local_blocks = jax.random.randint(jax.random.fold_in(key, 102), (N_SEQ, NB), 0, BPD)
    return (owners * BPD + local_blocks).astype(jnp.int32)


def key_table(key):
    base_rows = jax.random.normal(jax.random.fold_in(key, 201), (NBLK, BLK, KVCOL), jnp.float32)
    return base_rows


def draw_block_map(key, part):
    return block_table(key)


def draw_block_count(key, part):
    counts = jax.random.randint(jax.random.fold_in(key, 103), (N_SEQ,), NB - NB // 4, NB + 1)
    fullest = jax.random.randint(jax.random.fold_in(key, 104), (), 0, N_SEQ)
    counts = jnp.where(jnp.arange(N_SEQ) == fullest, NB, counts)
    return counts.astype(jnp.int32)


def draw_keys(key, part):
    return key_table(key).astype(jnp.bfloat16)


def draw_queries(key, part):
    query_rows = jax.random.normal(jax.random.fold_in(key, 301), (TEXT, HCOL), jnp.float32)
    query_rows = jnp.clip(query_rows, -6.0, 6.0)
    return query_rows.astype(jnp.bfloat16)


def levels(key, dims, pieces, low, high):
    gain = 1.0
    for position, parts in pieces:
        heights = jax.random.uniform(jax.random.fold_in(jax.random.fold_in(key, 6), position), (parts,), jnp.float32, low / len(pieces), high / len(pieces))
        gain = gain * jnp.repeat(jnp.exp(heights), dims[position] // parts).reshape((-1,) + (1,) * (len(dims) - 1 - position))
    return gain


def centred(own_key, extent, scale, limit, pieces=(), kind=jnp.bfloat16):
    drawn = scale * jax.random.normal(own_key, extent, jnp.float32)
    if pieces:
        drawn = drawn * levels(own_key, extent, pieces, -0.22, 0.18)
    return jnp.clip(drawn, -limit, limit).astype(kind)


def setup_inputs(seed: int = 0) -> dict:
    key_of = jax.random.split(jax.random.key(seed), 7)
    return {
        "queries": draw_queries(jax.random.fold_in(key_of[6], 71), 0),
        "keys": draw_keys(jax.random.fold_in(key_of[6], 71), 0),
        "values": centred(key_of[2], (NBLK, BLK, KVCOL), 1.0, 6.0, ((0, 64), (1, 8))),
        "grad_out": centred(key_of[3], (TEXT, HCOL), 1.0, 6.0, ((0, 64), (1, 8))),
        "block_map": draw_block_map(jax.random.fold_in(key_of[6], 71), 0),
        "block_count": draw_block_count(jax.random.fold_in(key_of[6], 71), 0),
    }


def reference(queries, keys, values, grad_out, block_map, block_count):
    score_scale = 1.0 / math.sqrt(HEAD_DIM)
    keys_per = NB * BLK

    def span(totals_in, span_id):
        total_keys, total_values = totals_in
        row_start = span_id * TOK_DEV
        q_rows = lax.dynamic_slice_in_dim(queries, row_start, TOK_DEV, 0).astype(jnp.float32).reshape(TOK_DEV, KV_HEADS, GROUP, HEAD_DIM)
        g_rows = lax.dynamic_slice_in_dim(grad_out, row_start, TOK_DEV, 0).astype(jnp.float32).reshape(TOK_DEV, KV_HEADS, GROUP, HEAD_DIM)
        row_ids = block_map[span_id].astype(jnp.int32)
        key_rows = keys[row_ids].astype(jnp.float32).reshape(keys_per, KV_HEADS, HEAD_DIM)
        value_rows = values[row_ids].astype(jnp.float32).reshape(keys_per, KV_HEADS, HEAD_DIM)
        live_blocks = jnp.arange(NB, dtype=jnp.int32) < block_count[span_id]
        key_live = jnp.repeat(live_blocks, BLK)
        scores = jnp.einsum('tgrd,kgd->grtk', q_rows, key_rows) * score_scale
        scores = jnp.where(key_live[None, None, None, :], scores, -1e+30)
        row_max = lax.optimization_barrier(jnp.max(scores, axis=3))
        weights = jnp.exp(scores - row_max[..., None])
        totals = lax.optimization_barrier(jnp.sum(weights, axis=3))
        probs_full = weights / totals[..., None]
        probs_low = lax.optimization_barrier(probs_full.astype(jnp.bfloat16)).astype(jnp.float32)
        context = jnp.einsum('grtk,kgd->tgrd', probs_low, value_rows)
        delta_row = lax.optimization_barrier(jnp.sum(g_rows * context, axis=3))
        value_part = jnp.einsum('grtk,tgrd->kgd', probs_low, g_rows)
        grad_probs = jnp.einsum('tgrd,kgd->grtk', g_rows, value_rows)
        grad_scores = probs_full * (grad_probs - jnp.transpose(delta_row, (1, 2, 0))[..., None])
        grad_scores = lax.optimization_barrier(grad_scores.astype(jnp.bfloat16)).astype(jnp.float32)
        grad_query = jnp.einsum('grtk,kgd->tgrd', grad_scores, key_rows) * score_scale
        key_part = jnp.einsum('grtk,tgrd->kgd', grad_scores, q_rows) * score_scale
        total_keys = total_keys.at[row_ids].add(key_part.reshape(NB, BLK, KVCOL))
        total_values = total_values.at[row_ids].add(value_part.reshape(NB, BLK, KVCOL))
        log_rows = (row_max + jnp.log(totals)).reshape(HEADS, TOK_DEV)
        return ((total_keys, total_values), (grad_query.reshape(TOK_DEV, HCOL).astype(jnp.bfloat16), log_rows))
    zeros = jnp.zeros((NBLK, BLK, KVCOL), jnp.float32)
    (sum_keys, sum_values), (grad_rows, log_rows) = lax.scan(span, (zeros, zeros), jnp.arange(N_SEQ, dtype=jnp.int32))
    log_totals = jnp.transpose(log_rows, (1, 0, 2)).reshape(HEADS, TEXT)
    return (grad_rows.reshape(TEXT, HCOL), log_totals, sum_keys.astype(jnp.bfloat16), sum_values.astype(jnp.bfloat16))
```

```python
import math

import jax
import jax.numpy as jnp
from jax import lax
from jax.experimental import pallas as pl
from jax.experimental.pallas import tpu as pltpu
from jax.sharding import PartitionSpec as P

HEAD_DIM = 128
GROUP = 8
N_X = 4
N_CORE = 2
MESH = pl.DeviceIdType.MESH
F32 = jnp.float32
BF16 = jnp.bfloat16


def rows_cols(left, right, dims):
    return lax.dot_general(left, right, (dims, ((), ())), preferred_element_type=F32)


def kernel(
    sizes,
    q_hbm,
    g_hbm,
    k_hbm,
    v_hbm,
    map_hbm,
    count_ref,
    dq_hbm,
    log_hbm,
    dk_hbm,
    dv_hbm,
    q_buf,
    g_buf,
    dq_buf,
    log_buf,
    own_rows,
    map_buf,
    land,
    table,
    pick_t,
    pack_t,
    chosen,
    got,
    kv_buf,
    part,
    part_in,
    terms,
    terms_in,
    sums,
    fin,
    out_rows,
    local_sem,
    send_sem,
    recv_sem,
):
    n_z, n_vis, per_owner, n_named, heads = sizes
    n_plane = N_X * n_vis
    seq = lax.axis_index("seq")
    vis = lax.axis_index("vis")
    z, x = seq // N_X, seq % N_X
    y, core = vis // N_CORE, vis % N_CORE
    place = x * n_vis + vis
    block = n_vis

    def plane_peer(step):
        where = (place + step) % n_plane
        return where // n_vis, where % n_vis

    def line_peer(step):
        back = (step + 1) // 2
        ahead = n_z // 2 + back * (1 - 2 * (step % 2))
        return (z + ahead) % n_z

    partner = (seq, y * N_CORE + 1 - core)

    barrier = pltpu.get_barrier_semaphore()

    def greet_line(step, carry):
        pl.semaphore_signal(
            barrier, inc=1, device_id=(line_peer(step) * N_X + x, vis), device_id_type=MESH
        )
        return carry

    def greet_plane(step, carry):
        px, pv = plane_peer(step)
        pl.semaphore_signal(barrier, inc=1, device_id=(z * N_X + px, pv), device_id_type=MESH)
        return carry

    lax.fori_loop(0, n_z - 1, greet_line, 0)
    lax.fori_loop(1, n_plane, greet_plane, 0)

    loads = [
        pltpu.make_async_copy(k_hbm, own_rows.at[0], local_sem.at[0]),
        pltpu.make_async_copy(v_hbm, own_rows.at[1], local_sem.at[1]),
        pltpu.make_async_copy(map_hbm, map_buf, local_sem.at[2]),
        pltpu.make_async_copy(q_hbm, q_buf, local_sem.at[3]),
        pltpu.make_async_copy(g_hbm, g_buf, local_sem.at[4]),
    ]
    for load in loads:
        load.start()
    loads[2].wait()

    block_ids = map_buf[...]
    n_seq = n_z * N_X
    owner_ids = block_ids // per_owner
    slot_ids = block_ids % per_owner
    wide = n_seq * block
    keys_n = n_named * block

    def iota(shape, axis):
        return lax.broadcasted_iota(jnp.int32, shape, axis)

    sub = iota((8, n_seq), 0)
    slots = jnp.zeros((8, n_seq), F32)
    for ox in range(N_X):
        slot = jnp.sum(
            jnp.where(owner_ids == z * N_X + ox, slot_ids, 0).astype(F32), axis=0, keepdims=True
        )
        slots = jnp.where(sub == ox, jnp.broadcast_to(slot, (8, n_seq)), slots)
    spread = jnp.where(
        iota((n_seq, wide), 0) == iota((n_seq, wide), 1) // (N_X * block) * N_X + x, 1.0, 0.0
    ).astype(BF16)
    slots = rows_cols(slots.astype(BF16), spread, ((1,), (0,)))
    lane_x = iota((8, wide), 1) // block % N_X
    slot_row = jnp.sum(jnp.where(iota((8, wide), 0) == lane_x, slots, 0.0), axis=0, keepdims=True)
    lane = iota((1, wide), 1)
    target = lane % block * (N_X * per_owner) + lane // block % N_X * per_owner
    target = target + slot_row.astype(jnp.int32)
    pick_t[...] = jnp.where(iota((n_plane * per_owner, wide), 0) == target, 1.0, 0.0).astype(BF16)

    my_owner = jnp.sum(
        jnp.where(iota((n_named, n_seq), 1) == seq, owner_ids, 0).astype(F32),
        axis=1,
        keepdims=True,
    )
    owner_row = jnp.sum(
        jnp.where(
            iota((n_named, keys_n), 0) == iota((n_named, keys_n), 1) // block,
            jnp.broadcast_to(my_owner, (n_named, keys_n)),
            0.0,
        ),
        axis=0,
        keepdims=True,
    )
    target = owner_row.astype(jnp.int32) * block + iota((1, keys_n), 1) % block
    pack_t[...] = jnp.where(iota((wide, keys_n), 0) == target, 1.0, 0.0).astype(BF16)

    loads[0].wait()
    loads[1].wait()
    pl.semaphore_wait(barrier, n_z - 1 + n_plane - 1)

    def piece(py, pc):
        return own_rows.at[pc, :, pl.ds(pl.multiple_of(py * HEAD_DIM, HEAD_DIM), HEAD_DIM)]

    here = vis * N_X + x

    def send_row(step, carry):
        px, pv = plane_peer(step)
        pltpu.make_async_remote_copy(
            src_ref=piece(pv // N_CORE, pv % N_CORE),
            dst_ref=land.at[here],
            send_sem=send_sem.at[0],
            recv_sem=recv_sem.at[0],
            device_id=(z * N_X + px, pv),
            device_id_type=MESH,
        ).start()
        return carry

    lax.fori_loop(1, n_plane, send_row, 0)
    keep = pltpu.make_async_copy(piece(y, core), land.at[here], local_sem.at[0])
    keep.start()
    keep.wait()

    def wait_bytes(ref, sem):
        pltpu.make_async_copy(ref, ref, sem).wait()

    wait_bytes(land.at[pl.ds(0, n_plane - 1)], recv_sem.at[0])
    for i in range(n_plane):
        table[i * per_owner : (i + 1) * per_owner, :] = land[i].astype(F32)

    line_rows = N_X * block
    chosen[...] = (
        rows_cols(pick_t[...], table[...].astype(BF16), ((0,), (0,)))
        .astype(BF16)
        .reshape(n_z, line_rows, HEAD_DIM)
    )

    def send_line(source, target_ref, slot):
        def body(step, carry):
            pz = line_peer(step)
            pltpu.make_async_remote_copy(
                src_ref=source.at[pz],
                dst_ref=target_ref.at[z],
                send_sem=send_sem.at[slot],
                recv_sem=recv_sem.at[slot],
                device_id=(pz * N_X + x, vis),
                device_id_type=MESH,
            ).start()
            return carry

        lax.fori_loop(0, n_z - 1, body, 0)
        own = pltpu.make_async_copy(source.at[z], target_ref.at[z], local_sem.at[0])
        own.start()
        own.wait()

    send_line(chosen, got, 1)
    wait_bytes(got.at[pl.ds(0, n_z - 1)], recv_sem.at[1])

    kv_buf[core] = rows_cols(
        pack_t[...], got[...].reshape(wide, HEAD_DIM), ((0,), (0,))
    ).astype(BF16)
    swap = pltpu.make_async_remote_copy(
        src_ref=kv_buf.at[core],
        dst_ref=kv_buf.at[core],
        send_sem=send_sem.at[2],
        recv_sem=recv_sem.at[2],
        device_id=partner,
        device_id_type=MESH,
    )
    swap.start()
    loads[3].wait()
    loads[4].wait()
    swap.wait()

    k_rows = kv_buf[0]
    v_rows = kv_buf[1]
    score_scale = 1.0 / math.sqrt(HEAD_DIM)
    live = lax.broadcasted_iota(jnp.int32, (keys_n, 1), 0) < count_ref[seq] * block
    dk = jnp.zeros((keys_n, HEAD_DIM), F32)
    dv = jnp.zeros((keys_n, HEAD_DIM), F32)
    for head in range(heads):
        cols = slice(head * HEAD_DIM, (head + 1) * HEAD_DIM)
        q_head = q_buf[:, cols]
        g_head = g_buf[:, cols]
        scores = rows_cols(k_rows, q_head, ((1,), (1,))) * score_scale
        scores = jnp.where(live, scores, -1e30)
        row_max = jnp.max(scores, axis=0, keepdims=True)
        weights = jnp.exp(scores - row_max)
        totals = jnp.sum(weights, axis=0, keepdims=True)
        log_buf[head : head + 1, :] = row_max + jnp.log(totals)
        probs = weights * (1.0 / totals)
        probs_low = probs.astype(BF16)
        grad_probs = rows_cols(v_rows, g_head, ((1,), (1,)))
        delta = jnp.sum(probs_low.astype(F32) * grad_probs, axis=0, keepdims=True)
        grad_scores = (probs * (grad_probs - delta)).astype(BF16)
        dv = dv + rows_cols(probs_low, g_head, ((1,), (0,)))
        dk = dk + rows_cols(grad_scores, q_head, ((1,), (0,)))
        dq_buf[:, cols] = (rows_cols(grad_scores, k_rows, ((0,), (0,))) * score_scale).astype(BF16)
    part[0] = dk * score_scale
    part[1] = dv

    give = pltpu.make_async_remote_copy(
        src_ref=part.at[1 - core],
        dst_ref=part_in,
        send_sem=send_sem.at[3],
        recv_sem=recv_sem.at[3],
        device_id=partner,
        device_id_type=MESH,
    )
    give.start()
    stores = [
        pltpu.make_async_copy(dq_buf, dq_hbm, local_sem.at[3]),
        pltpu.make_async_copy(log_buf, log_hbm, local_sem.at[4]),
    ]
    for store in stores:
        store.start()
    give.wait()
    both = (part[core] + part_in[...]).astype(BF16)
    terms[...] = (
        rows_cols(pack_t[...], both, ((1,), (0,)))
        .astype(BF16)
        .reshape(n_z, line_rows, HEAD_DIM)
    )
    send_line(terms, terms_in, 4)
    wait_bytes(terms_in.at[pl.ds(0, n_z - 1)], recv_sem.at[4])

    line_sum = rows_cols(pick_t[...], terms_in[...].reshape(wide, HEAD_DIM), ((1,), (0,)))
    for i in range(n_plane):
        sums[i] = line_sum[i * per_owner : (i + 1) * per_owner, :]

    def send_sum(step, carry):
        px, pv = plane_peer(step)
        pltpu.make_async_remote_copy(
            src_ref=sums.at[pv * N_X + px],
            dst_ref=fin.at[place],
            send_sem=send_sem.at[5],
            recv_sem=recv_sem.at[5],
            device_id=(z * N_X + px, pv),
            device_id_type=MESH,
        ).start()
        return carry

    lax.fori_loop(1, n_plane, send_sum, 0)
    last = pltpu.make_async_copy(sums.at[here], fin.at[place], local_sem.at[0])
    last.start()
    last.wait()
    wait_bytes(fin.at[pl.ds(0, n_plane - 1)], recv_sem.at[5])
    for pv in range(n_vis):
        total = fin[pv]
        for px in range(1, N_X):
            total = total + fin[px * n_vis + pv]
        low = (pv // N_CORE) * HEAD_DIM
        out_rows[pv % N_CORE, :, low : low + HEAD_DIM] = total.astype(BF16)
    ends = [
        pltpu.make_async_copy(out_rows.at[0], dk_hbm, local_sem.at[1]),
        pltpu.make_async_copy(out_rows.at[1], dv_hbm, local_sem.at[2]),
    ]
    for end in ends:
        end.start()
    wait_bytes(land.at[pl.ds(0, n_plane - 1)], send_sem.at[0])
    wait_bytes(got.at[pl.ds(0, n_z - 1)], send_sem.at[1])
    wait_bytes(terms_in.at[pl.ds(0, n_z - 1)], send_sem.at[4])
    wait_bytes(fin.at[pl.ds(0, n_plane - 1)], send_sem.at[5])
    for store in stores + ends:
        store.wait()


def local(queries, keys, values, grad_out, block_map, block_count):
    n_seq = lax.axis_size("seq")
    n_vis = lax.axis_size("vis")
    n_z = n_seq // N_X
    per_owner = keys.shape[0]
    width = keys.shape[2]
    n_named = block_map.shape[1]
    tokens, cols = queries.shape
    heads = cols // HEAD_DIM
    n_plane = N_X * n_vis
    keys_n = n_named * n_vis
    wide = n_seq * n_vis
    line = (n_z, N_X * n_vis, HEAD_DIM)
    any_spec = pl.BlockSpec(memory_space=pl.ANY)
    dq, log_totals, dk, dv = pl.pallas_call(
        lambda *refs: kernel((n_z, n_vis, per_owner, n_named, heads), *refs),
        name="block_attention",
        out_shape=(
            jax.ShapeDtypeStruct(queries.shape, BF16),
            jax.ShapeDtypeStruct((heads, tokens), F32),
            jax.ShapeDtypeStruct((per_owner, width), BF16),
            jax.ShapeDtypeStruct((per_owner, width), BF16),
        ),
        in_specs=[any_spec] * 5 + [pl.BlockSpec(memory_space=pltpu.SMEM)],
        out_specs=(any_spec,) * 4,
        scratch_shapes=[
            pltpu.VMEM((tokens, cols), BF16),
            pltpu.VMEM((tokens, cols), BF16),
            pltpu.VMEM((tokens, cols), BF16),
            pltpu.VMEM((heads, tokens), F32),
            pltpu.VMEM((2, per_owner, width), BF16),
            pltpu.VMEM(block_map.shape[::-1], jnp.int32),
            pltpu.VMEM((n_plane, per_owner, HEAD_DIM), BF16),
            pltpu.VMEM((n_plane * per_owner, HEAD_DIM), F32),
            pltpu.VMEM((n_plane * per_owner, wide), BF16),
            pltpu.VMEM((wide, keys_n), BF16),
            pltpu.VMEM(line, BF16),
            pltpu.VMEM(line, BF16),
            pltpu.VMEM((2, keys_n, HEAD_DIM), BF16),
            pltpu.VMEM((2, keys_n, HEAD_DIM), F32),
            pltpu.VMEM((keys_n, HEAD_DIM), F32),
            pltpu.VMEM(line, BF16),
            pltpu.VMEM(line, BF16),
            pltpu.VMEM((n_plane, per_owner, HEAD_DIM), F32),
            pltpu.VMEM((n_plane, per_owner, HEAD_DIM), F32),
            pltpu.VMEM((2, per_owner, width), BF16),
            pltpu.SemaphoreType.DMA((5,)),
            pltpu.SemaphoreType.DMA((6,)),
            pltpu.SemaphoreType.DMA((6,)),
        ],
        compiler_params=pltpu.CompilerParams(collective_id=0, has_side_effects=True),
    )(
        queries,
        grad_out,
        keys.reshape(per_owner, width),
        values.reshape(per_owner, width),
        block_map.T,
        block_count,
    )
    return (dq, log_totals, dk.reshape(keys.shape), dv.reshape(values.shape))


def solution(mesh):
    in_specs = (
        P("seq", "vis"),
        P("seq", "vis", None),
        P("seq", "vis", None),
        P("seq", "vis"),
        P(),
        P(),
    )
    out_specs = (P("seq", "vis"), P("vis", "seq"), P("seq", "vis", None), P("seq", "vis", None))
    return jax.shard_map(local, mesh=mesh, in_specs=in_specs, out_specs=out_specs, check_vma=False)
```

```python
import math

import jax
import jax.numpy as jnp
from jax import lax
from jax.experimental import pallas as pl
from jax.experimental.pallas import tpu as pltpu
from jax.sharding import PartitionSpec as P

HEAD_DIM = 128
GROUP = 8
N_X = 4
N_CORE = 2
CHUNKS = 4
MESH = pl.DeviceIdType.MESH
F32 = jnp.float32
BF16 = jnp.bfloat16


def rows_cols(left, right, dims):
    return lax.dot_general(left, right, (dims, ((), ())), preferred_element_type=F32)


def iota(shape, axis):
    return lax.broadcasted_iota(jnp.int32, shape, axis)


def mod(a, n):
    return lax.rem(a, jnp.int32(n))


def div(a, n):
    return lax.div(a, jnp.int32(n))


def kernel(
    sizes,
    q_hbm,
    g_hbm,
    k_hbm,
    v_hbm,
    map_hbm,
    count_ref,
    dq_ref,
    log_ref,
    out_rows,
    q_buf,
    g_buf,
    own_rows,
    map_buf,
    land,
    table,
    pick_t,
    pack_t,
    chosen,
    got,
    kv_buf,
    part,
    part_in,
    terms,
    terms_in,
    sums,
    fin,
    local_sem,
    send_sem,
    recv_sem,
    ready_sem,
):
    n_z, n_vis, per_owner, n_named, heads = sizes
    n_plane = N_X * n_vis
    n_chip_y = n_vis // N_CORE
    seq = lax.axis_index("seq")
    vis = lax.axis_index("vis")
    z, x = div(seq, N_X), mod(seq, N_X)
    y, core = div(vis, N_CORE), mod(vis, N_CORE)
    block = n_vis
    n_seq = n_z * N_X
    wide = n_seq * block
    keys_n = n_named * block
    line_rows = N_X * block

    half = n_z // 2
    order = [
        (half + (p + 1) // 2 * (1 - 2 * (p % 2))) % n_z for p in range(n_z)
    ]
    place_of = {d: p for p, d in enumerate(order)}
    line_seq = [mod(z + d, n_z) * N_X + x for d in range(n_z)]
    plane_seq = [z * N_X + mod(x + d, N_X) for d in range(N_X)]
    plane_vis = [mod(vis + d, n_vis) for d in range(n_vis)]
    far_x = sorted(range(N_X), key=lambda d: -min(d, N_X - d))
    far_v = sorted(range(n_vis), key=lambda d: -min(d, n_vis - d))
    plane = [(dx, dv) for dx in far_x for dv in far_v if dx or dv]
    partner = (seq, y * N_CORE + 1 - core)

    barrier = pltpu.get_barrier_semaphore()

    def greet(device):
        pl.semaphore_signal(barrier, inc=1, device_id=device, device_id_type=MESH)

    for d in order[:-1]:
        greet((line_seq[d], y * N_CORE + 1))
    chip_vis = [mod(y + d, n_chip_y) * N_CORE for d in range(n_chip_y)]
    for dx in far_x:
        for dy in range(n_chip_y):
            if dx or dy:
                greet((plane_seq[dx], chip_vis[dy]))
    greet(partner)

    loads = [
        pltpu.make_async_copy(k_hbm, own_rows.at[0], local_sem.at[0]),
        pltpu.make_async_copy(v_hbm, own_rows.at[1], local_sem.at[1]),
        pltpu.make_async_copy(map_hbm, map_buf, local_sem.at[2]),
        pltpu.make_async_copy(q_hbm, q_buf, local_sem.at[3]),
        pltpu.make_async_copy(g_hbm, g_buf, local_sem.at[4]),
    ]
    for load in loads:
        load.start()

    def wait_bytes(ref, sem):
        pltpu.make_async_copy(ref, ref, sem).wait()

    loads[0].wait()
    loads[1].wait()

    @pl.when(core == 0)
    def _():
        pl.semaphore_wait(barrier, n_plane - 1)
        pl.semaphore_signal(ready_sem, inc=1, device_id=partner, device_id_type=MESH)

    @pl.when(core == 1)
    def _():
        pl.semaphore_wait(ready_sem, 1)

    def piece(where):
        low = pl.multiple_of(div(where, N_CORE) * HEAD_DIM, HEAD_DIM)
        return own_rows.at[mod(where, N_CORE), :, pl.ds(low, HEAD_DIM)]

    pieces = [piece(where) for where in plane_vis]
    for dx, dv in plane:
        slot = (n_vis - dv) % n_vis * N_X + (N_X - dx) % N_X
        pltpu.make_async_remote_copy(
            src_ref=pieces[dv],
            dst_ref=land.at[slot],
            send_sem=send_sem.at[0],
            recv_sem=recv_sem.at[0],
            device_id=(plane_seq[dx], plane_vis[dv]),
            device_id_type=MESH,
        ).start()

    loads[2].wait()
    block_ids = map_buf[...]
    owner_ids = div(block_ids, per_owner)
    slot_ids = mod(block_ids, per_owner)
    sub = iota((8, n_seq), 0)
    slots = jnp.zeros((8, n_seq), F32)
    for ox in range(N_X):
        slot = jnp.sum(
            jnp.where(owner_ids == z * N_X + ox, slot_ids, 0).astype(F32), axis=0, keepdims=True
        )
        slots = jnp.where(sub == ox, jnp.broadcast_to(slot, (8, n_seq)), slots)
    lane = iota((1, wide), 1)
    lane_p = div(lane, N_X * block)
    lane_d = half + div(lane_p + 1, 2) * (1 - 2 * mod(lane_p, 2))
    lane_span = mod(z + lane_d, n_z) * N_X + x
    lane_x = mod(div(lane, block), N_X)
    spread = jnp.where(iota((n_seq, wide), 0) == lane_span, 1.0, 0.0).astype(BF16)
    slots = rows_cols(slots.astype(BF16), spread, ((1,), (0,)))
    slot_row = jnp.sum(jnp.where(iota((8, wide), 0) == lane_x, slots, 0.0), axis=0, keepdims=True)
    target = mod(mod(lane, block) + n_vis - vis, n_vis) * (N_X * per_owner)
    target = target + mod(lane_x + N_X - x, N_X) * per_owner + slot_row.astype(jnp.int32)
    pick_t[...] = jnp.where(iota((n_plane * per_owner, wide), 0) == target, 1.0, 0.0).astype(BF16)

    my_owner = jnp.sum(
        jnp.where(iota((n_named, n_seq), 1) == seq, owner_ids, 0).astype(F32),
        axis=1,
        keepdims=True,
    )
    owner_row = jnp.sum(
        jnp.where(
            iota((n_named, keys_n), 0) == div(iota((n_named, keys_n), 1), block),
            jnp.broadcast_to(my_owner, (n_named, keys_n)),
            0.0,
        ),
        axis=0,
        keepdims=True,
    ).astype(jnp.int32)
    away = mod(div(owner_row, N_X) + n_z - z, n_z) - half
    owner_p = jnp.where(away >= 0, 2 * away, -2 * away - 1)
    target = (owner_p * N_X + mod(owner_row, N_X)) * block + mod(iota((1, keys_n), 1), block)
    pack_t[...] = jnp.where(iota((wide, keys_n), 0) == target, 1.0, 0.0).astype(BF16)

    @pl.when(core == 1)
    def _():
        pl.semaphore_wait(barrier, N_CORE * (n_z - 1) + 1)
        pl.semaphore_signal(ready_sem, inc=1, device_id=partner, device_id_type=MESH)

    @pl.when(core == 0)
    def _():
        pl.semaphore_wait(ready_sem, 1)

    wait_bytes(land.at[pl.ds(1, n_plane - 1)], recv_sem.at[0])
    table[0:per_owner, :] = own_rows[
        core, :, pl.ds(pl.multiple_of(y * HEAD_DIM, HEAD_DIM), HEAD_DIM)
    ].astype(F32)
    for i in range(1, n_plane):
        table[i * per_owner : (i + 1) * per_owner, :] = land[i].astype(F32)

    per_chunk = n_z // CHUNKS

    def send_line(make_chunk, source, target_ref, index):
        for chunk in range(CHUNKS):
            first = chunk * per_chunk
            rows = make_chunk(first * line_rows, (first + per_chunk) * line_rows)
            rows = rows.astype(BF16).reshape(per_chunk, line_rows, HEAD_DIM)
            source[first : first + per_chunk] = rows
            for p in range(first, first + per_chunk):
                d = order[p]
                if d == 0:
                    target_ref[p] = rows[p - first]
                    continue
                pltpu.make_async_remote_copy(
                    src_ref=source.at[p],
                    dst_ref=target_ref.at[place_of[(n_z - d) % n_z]],
                    send_sem=send_sem.at[index],
                    recv_sem=recv_sem.at[index],
                    device_id=(line_seq[d], vis),
                    device_id_type=MESH,
                ).start()

    rows_in = table[...].astype(BF16)
    send_line(
        lambda low, high: rows_cols(pick_t[:, low:high], rows_in, ((0,), (0,))), chosen, got, 1
    )
    wait_bytes(got.at[pl.ds(0, n_z - 1)], recv_sem.at[1])

    kv_buf[core] = rows_cols(
        pack_t[...], got[...].reshape(wide, HEAD_DIM), ((0,), (0,))
    ).astype(BF16)
    swap = pltpu.make_async_remote_copy(
        src_ref=kv_buf.at[core],
        dst_ref=kv_buf.at[core],
        send_sem=send_sem.at[2],
        recv_sem=recv_sem.at[2],
        device_id=partner,
        device_id_type=MESH,
    )
    swap.start()
    loads[3].wait()
    loads[4].wait()
    swap.wait()

    k_rows = kv_buf[0]
    v_rows = kv_buf[1]
    score_scale = 1.0 / math.sqrt(HEAD_DIM)
    live = iota((keys_n, 1), 0) < count_ref[seq] * block
    dk = jnp.zeros((keys_n, HEAD_DIM), F32)
    dv = jnp.zeros((keys_n, HEAD_DIM), F32)
    for head in range(heads):
        cols = slice(head * HEAD_DIM, (head + 1) * HEAD_DIM)
        q_head = q_buf[:, cols]
        g_head = g_buf[:, cols]
        scores = rows_cols(k_rows, q_head, ((1,), (1,))) * score_scale
        scores = jnp.where(live, scores, -1e30)
        row_max = jnp.max(scores, axis=0, keepdims=True)
        weights = jnp.exp(scores - row_max)
        totals = jnp.sum(weights, axis=0, keepdims=True)
        log_ref[head : head + 1, :] = row_max + jnp.log(totals)
        probs = weights * (1.0 / totals)
        probs_low = probs.astype(BF16)
        grad_probs = rows_cols(v_rows, g_head, ((1,), (1,)))
        delta = jnp.sum(probs_low.astype(F32) * grad_probs, axis=0, keepdims=True)
        grad_scores = (probs * (grad_probs - delta)).astype(BF16)
        dv = dv + rows_cols(probs_low, g_head, ((1,), (0,)))
        dk = dk + rows_cols(grad_scores, q_head, ((1,), (0,)))
        dq_ref[:, cols] = (rows_cols(grad_scores, k_rows, ((0,), (0,))) * score_scale).astype(BF16)
    part[0] = dk * score_scale
    part[1] = dv

    give = pltpu.make_async_remote_copy(
        src_ref=part.at[1 - core],
        dst_ref=part_in,
        send_sem=send_sem.at[3],
        recv_sem=recv_sem.at[3],
        device_id=partner,
        device_id_type=MESH,
    )
    give.start()
    give.wait()
    both = (part[core] + part_in[...]).astype(BF16)
    send_line(
        lambda low, high: rows_cols(pack_t[low:high, :], both, ((1,), (0,))), terms, terms_in, 4
    )
    wait_bytes(terms_in.at[pl.ds(0, n_z - 1)], recv_sem.at[4])

    line_sum = rows_cols(pick_t[...], terms_in[...].reshape(wide, HEAD_DIM), ((1,), (0,)))
    for i in range(1, n_plane):
        sums[i] = line_sum[i * per_owner : (i + 1) * per_owner, :]
    fin[0, vis] = line_sum[0:per_owner, :]
    for dx, dv_step in plane:
        pltpu.make_async_remote_copy(
            src_ref=sums.at[dv_step * N_X + dx],
            dst_ref=fin.at[(N_X - dx) % N_X, vis],
            send_sem=send_sem.at[5],
            recv_sem=recv_sem.at[5],
            device_id=(plane_seq[dx], plane_vis[dv_step]),
            device_id_type=MESH,
        ).start()
    wait_bytes(sums.at[pl.ds(1, n_plane - 1)], recv_sem.at[5])
    for pv in range(n_vis):
        total = fin[0, pv]
        for px in range(1, N_X):
            total = total + fin[px, pv]
        low = (pv // N_CORE) * HEAD_DIM
        out_rows[pv % N_CORE, :, low : low + HEAD_DIM] = total.astype(BF16)
    wait_bytes(land.at[pl.ds(1, n_plane - 1)], send_sem.at[0])
    wait_bytes(got.at[pl.ds(0, n_z - 1)], send_sem.at[1])
    wait_bytes(terms_in.at[pl.ds(0, n_z - 1)], send_sem.at[4])
    wait_bytes(sums.at[pl.ds(1, n_plane - 1)], send_sem.at[5])


def write_out(dq_ref, log_ref, rows_ref, dq_hbm, log_hbm, dk_hbm, dv_hbm, sem):
    copies = [
        pltpu.make_async_copy(dq_ref, dq_hbm, sem.at[0]),
        pltpu.make_async_copy(log_ref, log_hbm, sem.at[1]),
        pltpu.make_async_copy(rows_ref.at[0], dk_hbm, sem.at[2]),
        pltpu.make_async_copy(rows_ref.at[1], dv_hbm, sem.at[3]),
    ]
    for copy in copies:
        copy.start()
    for copy in copies:
        copy.wait()


def local(queries, keys, values, grad_out, block_map, block_count):
    n_seq = lax.axis_size("seq")
    n_vis = lax.axis_size("vis")
    n_z = n_seq // N_X
    per_owner = keys.shape[0]
    width = keys.shape[2]
    n_named = block_map.shape[1]
    tokens, cols = queries.shape
    heads = cols // HEAD_DIM
    n_plane = N_X * n_vis
    keys_n = n_named * n_vis
    wide = n_seq * n_vis
    line = (n_z, N_X * n_vis, HEAD_DIM)
    any_spec = pl.BlockSpec(memory_space=pl.ANY)
    vmem_spec = pl.BlockSpec(memory_space=pltpu.VMEM)
    results = pl.pallas_call(
        lambda *refs: kernel((n_z, n_vis, per_owner, n_named, heads), *refs),
        name="block_attention",
        out_shape=(
            pltpu.VMEM(queries.shape, BF16),
            pltpu.VMEM((heads, tokens), F32),
            pltpu.VMEM((2, per_owner, width), BF16),
        ),
        in_specs=[any_spec] * 5 + [pl.BlockSpec(memory_space=pltpu.SMEM)],
        out_specs=(vmem_spec,) * 3,
        scratch_shapes=[
            pltpu.VMEM((tokens, cols), BF16),
            pltpu.VMEM((tokens, cols), BF16),
            pltpu.VMEM((2, per_owner, width), BF16),
            pltpu.VMEM(block_map.shape[::-1], jnp.int32),
            pltpu.VMEM((n_plane, per_owner, HEAD_DIM), BF16),
            pltpu.VMEM((n_plane * per_owner, HEAD_DIM), F32),
            pltpu.VMEM((n_plane * per_owner, wide), BF16),
            pltpu.VMEM((wide, keys_n), BF16),
            pltpu.VMEM(line, BF16),
            pltpu.VMEM(line, BF16),
            pltpu.VMEM((2, keys_n, HEAD_DIM), BF16),
            pltpu.VMEM((2, keys_n, HEAD_DIM), F32),
            pltpu.VMEM((keys_n, HEAD_DIM), F32),
            pltpu.VMEM(line, BF16),
            pltpu.VMEM(line, BF16),
            pltpu.VMEM((n_plane, per_owner, HEAD_DIM), F32),
            pltpu.VMEM((N_X, n_vis, per_owner, HEAD_DIM), F32),
            pltpu.SemaphoreType.DMA((5,)),
            pltpu.SemaphoreType.DMA((6,)),
            pltpu.SemaphoreType.DMA((6,)),
            pltpu.SemaphoreType.REGULAR,
        ],
        compiler_params=pltpu.CompilerParams(collective_id=0, has_side_effects=True),
    )(
        queries,
        grad_out,
        keys.reshape(per_owner, width),
        values.reshape(per_owner, width),
        block_map.T,
        block_count,
    )
    dq, log_totals, dk, dv = pl.pallas_call(
        write_out,
        name="write_out",
        out_shape=(
            jax.ShapeDtypeStruct(queries.shape, BF16),
            jax.ShapeDtypeStruct((heads, tokens), F32),
            jax.ShapeDtypeStruct((per_owner, width), BF16),
            jax.ShapeDtypeStruct((per_owner, width), BF16),
        ),
        in_specs=[vmem_spec] * 3,
        out_specs=(any_spec,) * 4,
        scratch_shapes=[pltpu.SemaphoreType.DMA((4,))],
    )(*[pltpu.with_memory_space_constraint(r, pltpu.VMEM) for r in results])
    return (dq, log_totals, dk.reshape(keys.shape), dv.reshape(values.shape))


def solution(mesh):
    in_specs = (
        P("seq", "vis"),
        P("seq", "vis", None),
        P("seq", "vis", None),
        P("seq", "vis"),
        P(),
        P(),
    )
    out_specs = (P("seq", "vis"), P("vis", "seq"), P("seq", "vis", None), P("seq", "vis", None))
    return jax.shard_map(local, mesh=mesh, in_specs=in_specs, out_specs=out_specs, check_vma=False)
```

```python
import math

import jax
import jax.numpy as jnp
from jax import lax
from jax.experimental import pallas as pl
from jax.experimental.pallas import tpu as pltpu
from jax.sharding import PartitionSpec as P

HEAD_DIM = 128
GROUP = 8
N_X = 4
N_CORE = 2
CHUNKS = 4
MESH = pl.DeviceIdType.MESH
F32 = jnp.float32
BF16 = jnp.bfloat16


def rows_cols(left, right, dims):
    return lax.dot_general(left, right, (dims, ((), ())), preferred_element_type=F32)


def iota(shape, axis):
    return lax.broadcasted_iota(jnp.int32, shape, axis)


def mod(a, n):
    return lax.rem(a, jnp.int32(n))


def div(a, n):
    return lax.div(a, jnp.int32(n))


def kernel(
    sizes,
    q_hbm,
    g_hbm,
    k_hbm,
    v_hbm,
    map_hbm,
    count_hbm,
    dq_ref,
    log_ref,
    out_rows,
    qg_buf,
    own_rows,
    map_buf,
    count_buf,
    first,
    ds_buf,
    land,
    table,
    pick_t,
    pack_t,
    chosen,
    got,
    kv_buf,
    part,
    part_in,
    terms,
    terms_in,
    sums,
    fin,
    local_sem,
    send_sem,
    recv_sem,
    ready_sem,
):
    n_z, n_vis, per_owner, n_named, heads = sizes
    n_plane = N_X * n_vis
    n_chip_y = n_vis // N_CORE
    seq = lax.axis_index("seq")
    vis = lax.axis_index("vis")
    z, x = div(seq, N_X), mod(seq, N_X)
    y, core = div(vis, N_CORE), mod(vis, N_CORE)
    block = n_vis
    n_seq = n_z * N_X
    wide = n_seq * block
    keys_n = n_named * block
    line_rows = N_X * block

    half = n_z // 2
    order = [
        (half + (p + 1) // 2 * (1 - 2 * (p % 2))) % n_z for p in range(n_z)
    ]
    place_of = {d: p for p, d in enumerate(order)}
    line_seq = [mod(z + d, n_z) * N_X + x for d in range(n_z)]
    plane_seq = [z * N_X + mod(x + d, N_X) for d in range(N_X)]
    plane_vis = [mod(vis + d, n_vis) for d in range(n_vis)]
    far_x = sorted(range(N_X), key=lambda d: -min(d, N_X - d))
    far_v = sorted(range(n_vis), key=lambda d: -min(d, n_vis - d))
    plane = [(dx, dv) for dx in far_x for dv in far_v if dx or dv]
    partner = (seq, y * N_CORE + 1 - core)

    loads = [
        pltpu.make_async_copy(k_hbm, own_rows.at[0], local_sem.at[0]),
        pltpu.make_async_copy(v_hbm, own_rows.at[1], local_sem.at[1]),
        pltpu.make_async_copy(map_hbm, map_buf, local_sem.at[2]),
        pltpu.make_async_copy(q_hbm, qg_buf.at[0], local_sem.at[3]),
        pltpu.make_async_copy(g_hbm, qg_buf.at[1], local_sem.at[4]),
        pltpu.make_async_copy(count_hbm, count_buf, local_sem.at[5]),
    ]
    for load in loads:
        load.start()

    barrier = pltpu.get_barrier_semaphore()

    def greet(device):
        pl.semaphore_signal(barrier, inc=1, device_id=device, device_id_type=MESH)

    for d in order[:-1]:
        greet((line_seq[d], y * N_CORE + 1))
    chip_vis = [mod(y + d, n_chip_y) * N_CORE for d in range(n_chip_y)]
    for dx in far_x:
        for dy in range(n_chip_y):
            if dx or dy:
                greet((plane_seq[dx], chip_vis[dy]))
    greet(partner)

    def wait_bytes(ref, sem):
        pltpu.make_async_copy(ref, ref, sem).wait()

    loads[0].wait()
    loads[1].wait()

    @pl.when(core == 0)
    def _():
        pl.semaphore_wait(barrier, n_plane - 1)
        pl.semaphore_signal(ready_sem, inc=1, device_id=partner, device_id_type=MESH)

    @pl.when(core == 1)
    def _():
        pl.semaphore_wait(ready_sem, 1)

    def piece(where):
        low = pl.multiple_of(div(where, N_CORE) * HEAD_DIM, HEAD_DIM)
        return own_rows.at[mod(where, N_CORE), :, pl.ds(low, HEAD_DIM)]

    pieces = [piece(where) for where in plane_vis]
    for dx, dv in plane:
        slot = (n_vis - dv) % n_vis * N_X + (N_X - dx) % N_X
        pltpu.make_async_remote_copy(
            src_ref=pieces[dv],
            dst_ref=land.at[slot],
            send_sem=send_sem.at[0],
            recv_sem=recv_sem.at[0],
            device_id=(plane_seq[dx], plane_vis[dv]),
            device_id_type=MESH,
        ).start()

    loads[2].wait()
    loads[5].wait()
    block_ids = map_buf[...]
    owner_ids = div(block_ids, per_owner)
    slot_ids = mod(block_ids, per_owner)
    sub = iota((8, n_seq), 0)
    slots = jnp.zeros((8, n_seq), F32)
    for ox in range(N_X):
        slot = jnp.sum(
            jnp.where(owner_ids == z * N_X + ox, slot_ids, 0).astype(F32), axis=0, keepdims=True
        )
        slots = jnp.where(sub == ox, jnp.broadcast_to(slot, (8, n_seq)), slots)
    lane = iota((1, wide), 1)
    lane_p = div(lane, N_X * block)
    lane_d = half + div(lane_p + 1, 2) * (1 - 2 * mod(lane_p, 2))
    lane_span = mod(z + lane_d, n_z) * N_X + x
    lane_x = mod(div(lane, block), N_X)
    spread = jnp.where(iota((n_seq, wide), 0) == lane_span, 1.0, 0.0).astype(BF16)
    slots = rows_cols(slots.astype(BF16), spread, ((1,), (0,)))
    slot_row = jnp.sum(jnp.where(iota((8, wide), 0) == lane_x, slots, 0.0), axis=0, keepdims=True)
    target = mod(mod(lane, block) + n_vis - vis, n_vis) * (N_X * per_owner)
    target = target + mod(lane_x + N_X - x, N_X) * per_owner + slot_row.astype(jnp.int32)
    pick_t[...] = jnp.where(iota((n_plane * per_owner, wide), 0) == target, 1.0, 0.0).astype(BF16)

    my_owner = jnp.sum(
        jnp.where(iota((n_named, n_seq), 1) == seq, owner_ids, 0).astype(F32),
        axis=1,
        keepdims=True,
    )
    owner_row = jnp.sum(
        jnp.where(
            iota((n_named, keys_n), 0) == div(iota((n_named, keys_n), 1), block),
            jnp.broadcast_to(my_owner, (n_named, keys_n)),
            0.0,
        ),
        axis=0,
        keepdims=True,
    ).astype(jnp.int32)
    away = mod(div(owner_row, N_X) + n_z - z, n_z) - half
    owner_p = jnp.where(away >= 0, 2 * away, -2 * away - 1)
    target = (owner_p * N_X + mod(owner_row, N_X)) * block + mod(iota((1, keys_n), 1), block)
    pack_t[...] = jnp.where(iota((wide, keys_n), 0) == target, 1.0, 0.0).astype(BF16)

    @pl.when(core == 1)
    def _():
        pl.semaphore_wait(barrier, N_CORE * (n_z - 1) + 1)
        pl.semaphore_signal(ready_sem, inc=1, device_id=partner, device_id_type=MESH)

    @pl.when(core == 0)
    def _():
        pl.semaphore_wait(ready_sem, 1)

    wait_bytes(land.at[pl.ds(1, n_plane - 1)], recv_sem.at[0])
    table[0:per_owner, :] = own_rows[
        core, :, pl.ds(pl.multiple_of(y * HEAD_DIM, HEAD_DIM), HEAD_DIM)
    ].astype(F32)
    for i in range(1, n_plane):
        table[i * per_owner : (i + 1) * per_owner, :] = land[i].astype(F32)

    per_chunk = n_z // CHUNKS

    def send_line(make_chunk, source, target_ref, index):
        for chunk in range(CHUNKS):
            first = chunk * per_chunk
            rows = make_chunk(first * line_rows, (first + per_chunk) * line_rows)
            rows = rows.astype(BF16).reshape(per_chunk, line_rows, HEAD_DIM)
            source[first : first + per_chunk] = rows
            for p in range(first, first + per_chunk):
                d = order[p]
                if d == 0:
                    target_ref[p] = rows[p - first]
                    continue
                pltpu.make_async_remote_copy(
                    src_ref=source.at[p],
                    dst_ref=target_ref.at[place_of[(n_z - d) % n_z]],
                    send_sem=send_sem.at[index],
                    recv_sem=recv_sem.at[index],
                    device_id=(line_seq[d], vis),
                    device_id_type=MESH,
                ).start()

    rows_in = table[...].astype(BF16)
    send_line(
        lambda low, high: rows_cols(pick_t[:, low:high], rows_in, ((0,), (0,))), chosen, got, 1
    )
    wait_bytes(got.at[pl.ds(0, n_z - 1)], recv_sem.at[1])

    kv_buf[core] = rows_cols(
        pack_t[...], got[...].reshape(wide, HEAD_DIM), ((0,), (0,))
    ).astype(BF16)
    swap = pltpu.make_async_remote_copy(
        src_ref=kv_buf.at[core],
        dst_ref=kv_buf.at[core],
        send_sem=send_sem.at[2],
        recv_sem=recv_sem.at[2],
        device_id=partner,
        device_id_type=MESH,
    )
    swap.start()
    loads[3].wait()
    loads[4].wait()

    def products(half):
        rows = kv_buf[half]
        for head in range(heads):
            cols = slice(head * HEAD_DIM, (head + 1) * HEAD_DIM)
            first[half, head] = rows_cols(rows, qg_buf[half, :, cols], ((1,), (1,)))

    products(core)
    swap.wait()
    products(1 - core)

    score_scale = 1.0 / math.sqrt(HEAD_DIM)
    my_count = jnp.sum(
        jnp.where(iota((1, n_seq), 1) == seq, count_buf[...], 0).astype(F32), axis=1, keepdims=True
    )
    live = iota((keys_n, 1), 0) < (my_count * block).astype(jnp.int32)
    dk = jnp.zeros((keys_n, HEAD_DIM), F32)
    dv = jnp.zeros((keys_n, HEAD_DIM), F32)
    for head in range(heads):
        cols = slice(head * HEAD_DIM, (head + 1) * HEAD_DIM)
        scores = jnp.where(live, first[0, head] * score_scale, -1e30)
        row_max = jnp.max(scores, axis=0, keepdims=True)
        weights = jnp.exp(scores - row_max)
        totals = jnp.sum(weights, axis=0, keepdims=True)
        log_ref[head : head + 1, :] = row_max + jnp.log(totals)
        probs = weights * (1.0 / totals)
        probs_low = probs.astype(BF16)
        grad_probs = first[1, head]
        delta = jnp.sum(probs_low.astype(F32) * grad_probs, axis=0, keepdims=True)
        grad_scores = (probs * (grad_probs - delta)).astype(BF16)
        ds_buf[head] = grad_scores
        dv = dv + rows_cols(probs_low, qg_buf[1, :, cols], ((1,), (0,)))
        dk = dk + rows_cols(grad_scores, qg_buf[0, :, cols], ((1,), (0,)))
    part[0] = dk * score_scale
    part[1] = dv

    give = pltpu.make_async_remote_copy(
        src_ref=part.at[1 - core],
        dst_ref=part_in,
        send_sem=send_sem.at[3],
        recv_sem=recv_sem.at[3],
        device_id=partner,
        device_id_type=MESH,
    )
    give.start()
    give.wait()
    both = (part[core] + part_in[...]).astype(BF16)
    send_line(
        lambda low, high: rows_cols(pack_t[low:high, :], both, ((1,), (0,))), terms, terms_in, 4
    )
    for head in range(heads):
        cols = slice(head * HEAD_DIM, (head + 1) * HEAD_DIM)
        dq = rows_cols(ds_buf[head], kv_buf[0], ((0,), (0,)))
        dq_ref[:, cols] = (dq * score_scale).astype(BF16)
    wait_bytes(terms_in.at[pl.ds(0, n_z - 1)], recv_sem.at[4])

    line_sum = rows_cols(pick_t[...], terms_in[...].reshape(wide, HEAD_DIM), ((1,), (0,)))
    for i in range(1, n_plane):
        sums[i] = line_sum[i * per_owner : (i + 1) * per_owner, :]
    fin[0, vis] = line_sum[0:per_owner, :]
    for dx, dv_step in plane:
        pltpu.make_async_remote_copy(
            src_ref=sums.at[dv_step * N_X + dx],
            dst_ref=fin.at[(N_X - dx) % N_X, vis],
            send_sem=send_sem.at[5],
            recv_sem=recv_sem.at[5],
            device_id=(plane_seq[dx], plane_vis[dv_step]),
            device_id_type=MESH,
        ).start()
    wait_bytes(sums.at[pl.ds(1, n_plane - 1)], recv_sem.at[5])
    for pv in range(n_vis):
        total = fin[0, pv]
        for px in range(1, N_X):
            total = total + fin[px, pv]
        low = (pv // N_CORE) * HEAD_DIM
        out_rows[pv % N_CORE, :, low : low + HEAD_DIM] = total.astype(BF16)
    wait_bytes(land.at[pl.ds(1, n_plane - 1)], send_sem.at[0])
    wait_bytes(got.at[pl.ds(0, n_z - 1)], send_sem.at[1])
    wait_bytes(terms_in.at[pl.ds(0, n_z - 1)], send_sem.at[4])
    wait_bytes(sums.at[pl.ds(1, n_plane - 1)], send_sem.at[5])


def write_out(dq_ref, log_ref, rows_ref, dq_hbm, log_hbm, dk_hbm, dv_hbm, sem):
    copies = [
        pltpu.make_async_copy(dq_ref, dq_hbm, sem.at[0]),
        pltpu.make_async_copy(log_ref, log_hbm, sem.at[1]),
        pltpu.make_async_copy(rows_ref.at[0], dk_hbm, sem.at[2]),
        pltpu.make_async_copy(rows_ref.at[1], dv_hbm, sem.at[3]),
    ]
    for copy in copies:
        copy.start()
    for copy in copies:
        copy.wait()


def local(queries, keys, values, grad_out, block_map, block_count):
    n_seq = lax.axis_size("seq")
    n_vis = lax.axis_size("vis")
    n_z = n_seq // N_X
    per_owner = keys.shape[0]
    width = keys.shape[2]
    n_named = block_map.shape[1]
    tokens, cols = queries.shape
    heads = cols // HEAD_DIM
    n_plane = N_X * n_vis
    keys_n = n_named * n_vis
    wide = n_seq * n_vis
    line = (n_z, N_X * n_vis, HEAD_DIM)
    any_spec = pl.BlockSpec(memory_space=pl.ANY)
    vmem_spec = pl.BlockSpec(memory_space=pltpu.VMEM)
    results = pl.pallas_call(
        lambda *refs: kernel((n_z, n_vis, per_owner, n_named, heads), *refs),
        name="block_attention",
        out_shape=(
            pltpu.VMEM(queries.shape, BF16),
            pltpu.VMEM((heads, tokens), F32),
            pltpu.VMEM((2, per_owner, width), BF16),
        ),
        in_specs=[any_spec] * 6,
        out_specs=(vmem_spec,) * 3,
        scratch_shapes=[
            pltpu.VMEM((2, tokens, cols), BF16),
            pltpu.VMEM((2, per_owner, width), BF16),
            pltpu.VMEM(block_map.shape[::-1], jnp.int32),
            pltpu.VMEM((1, n_seq), jnp.int32),
            pltpu.VMEM((2, heads, keys_n, tokens), F32),
            pltpu.VMEM((heads, keys_n, tokens), BF16),
            pltpu.VMEM((n_plane, per_owner, HEAD_DIM), BF16),
            pltpu.VMEM((n_plane * per_owner, HEAD_DIM), F32),
            pltpu.VMEM((n_plane * per_owner, wide), BF16),
            pltpu.VMEM((wide, keys_n), BF16),
            pltpu.VMEM(line, BF16),
            pltpu.VMEM(line, BF16),
            pltpu.VMEM((2, keys_n, HEAD_DIM), BF16),
            pltpu.VMEM((2, keys_n, HEAD_DIM), F32),
            pltpu.VMEM((keys_n, HEAD_DIM), F32),
            pltpu.VMEM(line, BF16),
            pltpu.VMEM(line, BF16),
            pltpu.VMEM((n_plane, per_owner, HEAD_DIM), F32),
            pltpu.VMEM((N_X, n_vis, per_owner, HEAD_DIM), F32),
            pltpu.SemaphoreType.DMA((6,)),
            pltpu.SemaphoreType.DMA((6,)),
            pltpu.SemaphoreType.DMA((6,)),
            pltpu.SemaphoreType.REGULAR,
        ],
        compiler_params=pltpu.CompilerParams(collective_id=0, has_side_effects=True),
    )(
        queries,
        grad_out,
        keys.reshape(per_owner, width),
        values.reshape(per_owner, width),
        block_map.T,
        block_count.reshape(1, n_seq),
    )
    dq, log_totals, dk, dv = pl.pallas_call(
        write_out,
        name="write_out",
        out_shape=(
            jax.ShapeDtypeStruct(queries.shape, BF16),
            jax.ShapeDtypeStruct((heads, tokens), F32),
            jax.ShapeDtypeStruct((per_owner, width), BF16),
            jax.ShapeDtypeStruct((per_owner, width), BF16),
        ),
        in_specs=[vmem_spec] * 3,
        out_specs=(any_spec,) * 4,
        scratch_shapes=[pltpu.SemaphoreType.DMA((4,))],
    )(*[pltpu.with_memory_space_constraint(r, pltpu.VMEM) for r in results])
    return (dq, log_totals, dk.reshape(keys.shape), dv.reshape(values.shape))


def solution(mesh):
    in_specs = (
        P("seq", "vis"),
        P("seq", "vis", None),
        P("seq", "vis", None),
        P("seq", "vis"),
        P(),
        P(),
    )
    out_specs = (P("seq", "vis"), P("vis", "seq"), P("seq", "vis", None), P("seq", "vis", None))
    return jax.shard_map(local, mesh=mesh, in_specs=in_specs, out_specs=out_specs, check_vma=False)
```

```python
import math

import jax
import jax.numpy as jnp
from jax import lax
from jax.experimental import pallas as pl
from jax.experimental.pallas import tpu as pltpu
from jax.sharding import PartitionSpec as P

HEAD_DIM = 128
GROUP = 8
N_X = 4
N_CORE = 2
CHUNKS = 4
MESH = pl.DeviceIdType.MESH
F32 = jnp.float32
BF16 = jnp.bfloat16


def rows_cols(left, right, dims):
    return lax.dot_general(left, right, (dims, ((), ())), preferred_element_type=F32)


def iota(shape, axis):
    return lax.broadcasted_iota(jnp.int32, shape, axis)


def mod(a, n):
    return lax.rem(a, jnp.int32(n))


def div(a, n):
    return lax.div(a, jnp.int32(n))


def kernel(
    sizes,
    q_hbm,
    g_hbm,
    k_hbm,
    v_hbm,
    map_hbm,
    count_hbm,
    dq_ref,
    log_ref,
    out_rows,
    qg_buf,
    own_rows,
    map_buf,
    count_buf,
    first,
    left,
    land,
    table,
    pick_t,
    pack_t,
    chosen,
    got,
    kv_buf,
    part,
    part_in,
    terms,
    terms_in,
    sums,
    fin,
    local_sem,
    send_sem,
    recv_sem,
    ready_sem,
):
    n_z, n_vis, per_owner, n_named, heads = sizes
    n_plane = N_X * n_vis
    n_chip_y = n_vis // N_CORE
    seq = lax.axis_index("seq")
    vis = lax.axis_index("vis")
    z, x = div(seq, N_X), mod(seq, N_X)
    y, core = div(vis, N_CORE), mod(vis, N_CORE)
    block = n_vis
    n_seq = n_z * N_X
    wide = n_seq * block
    keys_n = n_named * block
    line_rows = N_X * block

    half = n_z // 2
    order = [
        (half + (p + 1) // 2 * (1 - 2 * (p % 2))) % n_z for p in range(n_z)
    ]
    place_of = {d: p for p, d in enumerate(order)}
    line_seq = [mod(z + d, n_z) * N_X + x for d in range(n_z)]
    plane_seq = [z * N_X + mod(x + d, N_X) for d in range(N_X)]
    plane_vis = [mod(vis + d, n_vis) for d in range(n_vis)]
    far_x = sorted(range(N_X), key=lambda d: -min(d, N_X - d))
    far_v = sorted(range(n_vis), key=lambda d: -min(d, n_vis - d))
    plane = [(dx, dv) for dx in far_x for dv in far_v if dx or dv]
    partner = (seq, y * N_CORE + 1 - core)

    loads = [
        pltpu.make_async_copy(k_hbm, own_rows.at[0], local_sem.at[0]),
        pltpu.make_async_copy(v_hbm, own_rows.at[1], local_sem.at[1]),
        pltpu.make_async_copy(map_hbm, map_buf, local_sem.at[2]),
        pltpu.make_async_copy(q_hbm, qg_buf.at[0], local_sem.at[3]),
        pltpu.make_async_copy(g_hbm, qg_buf.at[1], local_sem.at[4]),
        pltpu.make_async_copy(count_hbm, count_buf, local_sem.at[5]),
    ]
    for load in loads:
        load.start()

    barrier = pltpu.get_barrier_semaphore()

    def greet(device):
        pl.semaphore_signal(barrier, inc=1, device_id=device, device_id_type=MESH)

    for d in order[:-1]:
        greet((line_seq[d], y * N_CORE + 1))
    chip_vis = [mod(y + d, n_chip_y) * N_CORE for d in range(n_chip_y)]
    for dx in far_x:
        for dy in range(n_chip_y):
            if dx or dy:
                greet((plane_seq[dx], chip_vis[dy]))
    greet(partner)

    def wait_bytes(ref, sem):
        pltpu.make_async_copy(ref, ref, sem).wait()

    loads[0].wait()
    loads[1].wait()

    @pl.when(core == 0)
    def _():
        pl.semaphore_wait(barrier, n_plane - 1)
        pl.semaphore_signal(ready_sem, inc=1, device_id=partner, device_id_type=MESH)

    @pl.when(core == 1)
    def _():
        pl.semaphore_wait(ready_sem, 1)

    def piece(where):
        low = pl.multiple_of(div(where, N_CORE) * HEAD_DIM, HEAD_DIM)
        return own_rows.at[mod(where, N_CORE), :, pl.ds(low, HEAD_DIM)]

    pieces = [piece(where) for where in plane_vis]
    for dx, dv in plane:
        slot = (n_vis - dv) % n_vis * N_X + (N_X - dx) % N_X
        pltpu.make_async_remote_copy(
            src_ref=pieces[dv],
            dst_ref=land.at[slot],
            send_sem=send_sem.at[0],
            recv_sem=recv_sem.at[0],
            device_id=(plane_seq[dx], plane_vis[dv]),
            device_id_type=MESH,
        ).start()

    loads[2].wait()
    loads[5].wait()
    block_ids = map_buf[...]
    owner_ids = div(block_ids, per_owner)
    slot_ids = mod(block_ids, per_owner)
    sub = iota((8, n_seq), 0)
    slots = jnp.zeros((8, n_seq), F32)
    for ox in range(N_X):
        slot = jnp.sum(
            jnp.where(owner_ids == z * N_X + ox, slot_ids, 0).astype(F32), axis=0, keepdims=True
        )
        slots = jnp.where(sub == ox, jnp.broadcast_to(slot, (8, n_seq)), slots)
    lane = iota((1, wide), 1)
    lane_p = div(lane, N_X * block)
    lane_d = half + div(lane_p + 1, 2) * (1 - 2 * mod(lane_p, 2))
    lane_span = mod(z + lane_d, n_z) * N_X + x
    lane_x = mod(div(lane, block), N_X)
    spread = jnp.where(iota((n_seq, wide), 0) == lane_span, 1.0, 0.0).astype(BF16)
    slots = rows_cols(slots.astype(BF16), spread, ((1,), (0,)))
    slot_row = jnp.sum(jnp.where(iota((8, wide), 0) == lane_x, slots, 0.0), axis=0, keepdims=True)
    target = mod(mod(lane, block) + n_vis - vis, n_vis) * (N_X * per_owner)
    target = target + mod(lane_x + N_X - x, N_X) * per_owner + slot_row.astype(jnp.int32)
    pick_t[...] = jnp.where(iota((n_plane * per_owner, wide), 0) == target, 1.0, 0.0).astype(BF16)

    my_owner = jnp.sum(
        jnp.where(iota((n_named, n_seq), 1) == seq, owner_ids, 0).astype(F32),
        axis=1,
        keepdims=True,
    )
    owner_row = jnp.sum(
        jnp.where(
            iota((n_named, keys_n), 0) == div(iota((n_named, keys_n), 1), block),
            jnp.broadcast_to(my_owner, (n_named, keys_n)),
            0.0,
        ),
        axis=0,
        keepdims=True,
    ).astype(jnp.int32)
    away = mod(div(owner_row, N_X) + n_z - z, n_z) - half
    owner_p = jnp.where(away >= 0, 2 * away, -2 * away - 1)
    target = (owner_p * N_X + mod(owner_row, N_X)) * block + mod(iota((1, keys_n), 1), block)
    pack_t[...] = jnp.where(iota((wide, keys_n), 0) == target, 1.0, 0.0).astype(BF16)

    @pl.when(core == 1)
    def _():
        pl.semaphore_wait(barrier, N_CORE * (n_z - 1) + 1)
        pl.semaphore_signal(ready_sem, inc=1, device_id=partner, device_id_type=MESH)

    @pl.when(core == 0)
    def _():
        pl.semaphore_wait(ready_sem, 1)

    wait_bytes(land.at[pl.ds(1, n_plane - 1)], recv_sem.at[0])
    table[0:per_owner, :] = own_rows[
        core, :, pl.ds(pl.multiple_of(y * HEAD_DIM, HEAD_DIM), HEAD_DIM)
    ].astype(F32)
    for i in range(1, n_plane):
        table[i * per_owner : (i + 1) * per_owner, :] = land[i].astype(F32)

    per_chunk = n_z // CHUNKS

    def send_line(make_chunk, source, target_ref, index):
        for chunk in range(CHUNKS):
            first = chunk * per_chunk
            rows = make_chunk(first * line_rows, (first + per_chunk) * line_rows)
            rows = rows.astype(BF16).reshape(per_chunk, line_rows, HEAD_DIM)
            source[first : first + per_chunk] = rows
            for p in range(first, first + per_chunk):
                d = order[p]
                if d == 0:
                    target_ref[p] = rows[p - first]
                    continue
                pltpu.make_async_remote_copy(
                    src_ref=source.at[p],
                    dst_ref=target_ref.at[place_of[(n_z - d) % n_z]],
                    send_sem=send_sem.at[index],
                    recv_sem=recv_sem.at[index],
                    device_id=(line_seq[d], vis),
                    device_id_type=MESH,
                ).start()

    rows_in = table[...].astype(BF16)
    send_line(
        lambda low, high: rows_cols(pick_t[:, low:high], rows_in, ((0,), (0,))), chosen, got, 1
    )
    wait_bytes(got.at[pl.ds(0, n_z - 1)], recv_sem.at[1])

    kv_buf[core] = rows_cols(
        pack_t[...], got[...].reshape(wide, HEAD_DIM), ((0,), (0,))
    ).astype(BF16)
    swap = pltpu.make_async_remote_copy(
        src_ref=kv_buf.at[core],
        dst_ref=kv_buf.at[core],
        send_sem=send_sem.at[2],
        recv_sem=recv_sem.at[2],
        device_id=partner,
        device_id_type=MESH,
    )
    swap.start()
    loads[3].wait()
    loads[4].wait()

    def products(half):
        rows = kv_buf[half]
        for head in range(heads):
            cols = slice(head * HEAD_DIM, (head + 1) * HEAD_DIM)
            first[half, head] = rows_cols(rows, qg_buf[half, :, cols], ((1,), (1,)))

    products(core)
    swap.wait()
    products(1 - core)

    score_scale = 1.0 / math.sqrt(HEAD_DIM)
    my_count = jnp.sum(
        jnp.where(iota((1, n_seq), 1) == seq, count_buf[...], 0).astype(F32), axis=1, keepdims=True
    )
    sure = n_named * 3 // 4 * block
    live = iota((keys_n - sure, 1), 0) + sure < (my_count * block).astype(jnp.int32)
    factor = score_scale / math.log(2.0)
    other = 1 - core
    given = jnp.zeros((keys_n, HEAD_DIM), F32)
    for head in range(heads):
        cols = slice(head * HEAD_DIM, (head + 1) * HEAD_DIM)
        scores = jnp.concatenate(
            [first[0, head, :sure], jnp.where(live, first[0, head, sure:], -1e30)], axis=0
        )
        row_max = jnp.max(scores, axis=0, keepdims=True)
        weights = jnp.exp2((scores - row_max) * factor)
        totals = jnp.sum(weights, axis=0, keepdims=True)
        log_ref[head : head + 1, :] = row_max * score_scale + jnp.log(totals)
        probs = weights * (1.0 / totals)
        probs_low = probs.astype(BF16)
        grad_probs = first[1, head]
        delta = jnp.sum(probs_low.astype(F32) * grad_probs, axis=0, keepdims=True)
        left[0, head] = (probs * (grad_probs - delta)).astype(BF16)
        left[1, head] = probs_low
        given = given + rows_cols(left[other, head], qg_buf[other, :, cols], ((1,), (0,)))

    part[...] = (given * jnp.where(core == 1, score_scale, 1.0)).astype(BF16)
    give = pltpu.make_async_remote_copy(
        src_ref=part,
        dst_ref=part_in,
        send_sem=send_sem.at[3],
        recv_sem=recv_sem.at[3],
        device_id=partner,
        device_id_type=MESH,
    )
    give.start()
    kept = jnp.zeros((keys_n, HEAD_DIM), F32)
    for head in range(heads):
        cols = slice(head * HEAD_DIM, (head + 1) * HEAD_DIM)
        kept = kept + rows_cols(left[core, head], qg_buf[core, :, cols], ((1,), (0,)))
    kept = kept * jnp.where(core == 0, score_scale, 1.0)
    give.wait()
    both = (kept + part_in[...].astype(F32)).astype(BF16)
    send_line(
        lambda low, high: rows_cols(pack_t[low:high, :], both, ((1,), (0,))), terms, terms_in, 4
    )
    for head in range(heads):
        cols = slice(head * HEAD_DIM, (head + 1) * HEAD_DIM)
        dq = rows_cols(left[0, head], kv_buf[0], ((0,), (0,)))
        dq_ref[:, cols] = (dq * score_scale).astype(BF16)
    wait_bytes(terms_in.at[pl.ds(0, n_z - 1)], recv_sem.at[4])

    line_sum = rows_cols(pick_t[...], terms_in[...].reshape(wide, HEAD_DIM), ((1,), (0,)))
    for i in range(1, n_plane):
        sums[i] = line_sum[i * per_owner : (i + 1) * per_owner, :]
    fin[0, vis] = line_sum[0:per_owner, :]
    for dx, dv_step in plane:
        pltpu.make_async_remote_copy(
            src_ref=sums.at[dv_step * N_X + dx],
            dst_ref=fin.at[(N_X - dx) % N_X, vis],
            send_sem=send_sem.at[5],
            recv_sem=recv_sem.at[5],
            device_id=(plane_seq[dx], plane_vis[dv_step]),
            device_id_type=MESH,
        ).start()
    wait_bytes(sums.at[pl.ds(1, n_plane - 1)], recv_sem.at[5])
    for pv in range(n_vis):
        total = fin[0, pv]
        for px in range(1, N_X):
            total = total + fin[px, pv]
        low = (pv // N_CORE) * HEAD_DIM
        out_rows[pv % N_CORE, :, low : low + HEAD_DIM] = total.astype(BF16)
    wait_bytes(land.at[pl.ds(1, n_plane - 1)], send_sem.at[0])
    wait_bytes(got.at[pl.ds(0, n_z - 1)], send_sem.at[1])
    wait_bytes(terms_in.at[pl.ds(0, n_z - 1)], send_sem.at[4])
    wait_bytes(sums.at[pl.ds(1, n_plane - 1)], send_sem.at[5])


def write_out(dq_ref, log_ref, rows_ref, dq_hbm, log_hbm, dk_hbm, dv_hbm, sem):
    copies = [
        pltpu.make_async_copy(dq_ref, dq_hbm, sem.at[0]),
        pltpu.make_async_copy(log_ref, log_hbm, sem.at[1]),
        pltpu.make_async_copy(rows_ref.at[0], dk_hbm, sem.at[2]),
        pltpu.make_async_copy(rows_ref.at[1], dv_hbm, sem.at[3]),
    ]
    for copy in copies:
        copy.start()
    for copy in copies:
        copy.wait()


def local(queries, keys, values, grad_out, block_map, block_count):
    n_seq = lax.axis_size("seq")
    n_vis = lax.axis_size("vis")
    n_z = n_seq // N_X
    per_owner = keys.shape[0]
    width = keys.shape[2]
    n_named = block_map.shape[1]
    tokens, cols = queries.shape
    heads = cols // HEAD_DIM
    n_plane = N_X * n_vis
    keys_n = n_named * n_vis
    wide = n_seq * n_vis
    line = (n_z, N_X * n_vis, HEAD_DIM)
    any_spec = pl.BlockSpec(memory_space=pl.ANY)
    vmem_spec = pl.BlockSpec(memory_space=pltpu.VMEM)
    results = pl.pallas_call(
        lambda *refs: kernel((n_z, n_vis, per_owner, n_named, heads), *refs),
        name="block_attention",
        out_shape=(
            pltpu.VMEM(queries.shape, BF16),
            pltpu.VMEM((heads, tokens), F32),
            pltpu.VMEM((2, per_owner, width), BF16),
        ),
        in_specs=[any_spec] * 6,
        out_specs=(vmem_spec,) * 3,
        scratch_shapes=[
            pltpu.VMEM((2, tokens, cols), BF16),
            pltpu.VMEM((2, per_owner, width), BF16),
            pltpu.VMEM(block_map.shape[::-1], jnp.int32),
            pltpu.VMEM((1, n_seq), jnp.int32),
            pltpu.VMEM((2, heads, keys_n, tokens), F32),
            pltpu.VMEM((2, heads, keys_n, tokens), BF16),
            pltpu.VMEM((n_plane, per_owner, HEAD_DIM), BF16),
            pltpu.VMEM((n_plane * per_owner, HEAD_DIM), F32),
            pltpu.VMEM((n_plane * per_owner, wide), BF16),
            pltpu.VMEM((wide, keys_n), BF16),
            pltpu.VMEM(line, BF16),
            pltpu.VMEM(line, BF16),
            pltpu.VMEM((2, keys_n, HEAD_DIM), BF16),
            pltpu.VMEM((keys_n, HEAD_DIM), BF16),
            pltpu.VMEM((keys_n, HEAD_DIM), BF16),
            pltpu.VMEM(line, BF16),
            pltpu.VMEM(line, BF16),
            pltpu.VMEM((n_plane, per_owner, HEAD_DIM), F32),
            pltpu.VMEM((N_X, n_vis, per_owner, HEAD_DIM), F32),
            pltpu.SemaphoreType.DMA((6,)),
            pltpu.SemaphoreType.DMA((6,)),
            pltpu.SemaphoreType.DMA((6,)),
            pltpu.SemaphoreType.REGULAR,
        ],
        compiler_params=pltpu.CompilerParams(collective_id=0, has_side_effects=True),
    )(
        queries,
        grad_out,
        keys.reshape(per_owner, width),
        values.reshape(per_owner, width),
        block_map.T,
        block_count.reshape(1, n_seq),
    )
    dq, log_totals, dk, dv = pl.pallas_call(
        write_out,
        name="write_out",
        out_shape=(
            jax.ShapeDtypeStruct(queries.shape, BF16),
            jax.ShapeDtypeStruct((heads, tokens), F32),
            jax.ShapeDtypeStruct((per_owner, width), BF16),
            jax.ShapeDtypeStruct((per_owner, width), BF16),
        ),
        in_specs=[vmem_spec] * 3,
        out_specs=(any_spec,) * 4,
        scratch_shapes=[pltpu.SemaphoreType.DMA((4,))],
    )(*[pltpu.with_memory_space_constraint(r, pltpu.VMEM) for r in results])
    return (dq, log_totals, dk.reshape(keys.shape), dv.reshape(values.shape))


def solution(mesh):
    in_specs = (
        P("seq", "vis"),
        P("seq", "vis", None),
        P("seq", "vis", None),
        P("seq", "vis"),
        P(),
        P(),
    )
    out_specs = (P("seq", "vis"), P("vis", "seq"), P("seq", "vis", None), P("seq", "vis", None))
    return jax.shard_map(local, mesh=mesh, in_specs=in_specs, out_specs=out_specs, check_vma=False)
```
